256 devices in a mesh: gx: 16 (over z_hi, y, core), gy: 16 (over x, z_lo).
Axes of the slice: x: 4, y: 4, z: 8 (z_hi: 2, z_lo: 4; z = z_hi * 4 + z_lo), core: 2. Of those that a mesh axis runs over, the one named last changes fastest.
Arguments:
- radiation: float32 [2, 4, 8, 256, 2048], P(None, None, None, 'gx', 'gy'), may hold values from -4 to 4, as said below
- ion_fraction: float32 [8, 256, 2048], P(None, 'gx', 'gy'), may hold values from 0.05 to 0.95
- density: float32 [8, 256, 2048], P(None, 'gx', 'gy'), may hold values from 0.1 to 10
- star_lum: float32 [16, 16, 2, 256], P('gx', 'gy'), may hold values from 0.1 to 10
- star_cell: int32 [16, 16, 3, 256], P('gx', 'gy'), may hold values from 0 to 127, as said below
- star_offset: float32 [16, 16, 3, 256], P('gx', 'gy'), may hold values from 0 to 1
- star_count: int32 [16, 16], P('gx', 'gy'), may hold values from 1 to 256, as said below
Outputs:
- radiation_out: float32 [2, 4, 8, 256, 2048], P(None, None, None, 'gx', 'gy')
- ion_out: float32 [8, 256, 2048], P(None, 'gx', 'gy')
The draws below stay inside these ranges and needn't reach their ends.
Inputs may be any that keep to these rules, and one draw needn't show every extreme that they name: `star_cell`: per slot: row 0 is the x corner within the tile, 0 to 15; row 1 the y corner, 0 to 127; row 2 the z corner, 0 to 7. `star_count`: some tile has all 256 slots live in every draw. `radiation`: N is positive and |F| < N in every cell.
All inputs are finite; a program needn't handle non-finite values.
Results may differ from the reference program's by a relative error of at most 0.0001.
Values sent between devices are 32-bit elements; how exact they have to be, the bound alone decides.
A program may use at most 64 MiB of HBM per device.

```python
import math
import jax
import jax.numpy as jnp
from jax import lax

G = 2
CX = 16
CY = 128
NZ = 8
S_DEV = 256
SUBSTEPS = 4
CHEM_ITERS = 3
NX = 256
NY = 2048
TILES_X = 16
TILES_Y = 16


def draw_radiation(key, part):
    key_n = jax.random.fold_in(key, 11)
    key_d = jax.random.fold_in(key, 12)
    key_r = jax.random.fold_in(key, 13)
    shape = (G, NZ, NX, NY)
    low, high, reach = (0.1, 2.0, 0.9)
    photons = jnp.exp(jax.random.uniform(key_n, shape, jnp.float32, jnp.log(low), jnp.log(high)))
    direction = jax.random.normal(key_d, (G, 3, NZ, NX, NY), jnp.float32)
    length = jnp.sqrt(jnp.sum(direction * direction, axis=1, keepdims=True)) + 1e-06
    ratio = jax.random.uniform(key_r, shape, jnp.float32, 0.0, reach)
    flux = direction / length * (photons * ratio)[:, None]
    return jnp.concatenate([photons[:, None], flux], axis=1)


def draw_star_cell(key, part):
    shape = (TILES_X, TILES_Y, S_DEV)
    xs = jax.random.randint(jax.random.fold_in(key, 21), shape, 0, CX)
    ys = jax.random.randint(jax.random.fold_in(key, 22), shape, 0, CY)
    zs = jax.random.randint(jax.random.fold_in(key, 23), shape, 0, NZ)
    return jnp.stack([xs, ys, zs], axis=2).astype(jnp.int32)


def draw_star_count(key, part):
    divisor = jax.random.randint(jax.random.fold_in(key, 31), (TILES_X * TILES_Y,), 1, 9)
    counts = S_DEV // divisor
    chosen = jax.random.randint(jax.random.fold_in(key, 32), (), 0, TILES_X * TILES_Y)
    counts = counts.at[chosen].set(S_DEV)
    return counts.reshape(TILES_X, TILES_Y).astype(jnp.int32)


def block_scale(key, shape, shards, low, top_value):
    level, own = 1.0, jax.random.fold_in(key, 6)
    for axis_at, blocks in shards:
        steps = jnp.exp(jax.random.uniform(jax.random.fold_in(own, axis_at), (blocks,), jnp.float32, low / len(shards), top_value / len(shards)))
        level = level * jnp.repeat(steps, shape[axis_at] // blocks).reshape([-1 if axis == axis_at else 1 for axis in range(len(shape))])
    return level


def setup_inputs(seed: int = 0) -> dict:
    seeds = jax.random.split(jax.random.key(seed), 8)
    return {
        "radiation": draw_radiation(jax.random.fold_in(seeds[7], 71), 0),
        "ion_fraction": jnp.clip(0.05 + 0.9 * jax.random.uniform(seeds[1], (NZ, NX, NY), jnp.float32) ** block_scale(seeds[1], (NZ, NX, NY), ((1, 16), (2, 16)), -0.2, 0.2), 0.05, 0.95),
        "density": jnp.clip(jnp.exp(math.log(10.0) - 4.6051702 * jax.random.uniform(seeds[2], (NZ, NX, NY), jnp.float32) ** block_scale(seeds[2], (NZ, NX, NY), ((1, 16), (2, 16)), -0.2, 0.2)), 0.1, 10.0),
        "star_lum": jnp.clip(jnp.exp(math.log(10.0) - 4.6051702 * jax.random.uniform(seeds[3], (TILES_X, TILES_Y, G, S_DEV), jnp.float32) ** block_scale(seeds[3], (TILES_X, TILES_Y, G, S_DEV), ((0, 16), (1, 16)), -0.2, 0.2)), 0.1, 10.0),
        "star_cell": draw_star_cell(jax.random.fold_in(seeds[7], 71), 0),
        "star_offset": jnp.clip(1.0 * jax.random.uniform(seeds[5], (TILES_X, TILES_Y, 3, S_DEV), jnp.float32) ** block_scale(seeds[5], (TILES_X, TILES_Y, 3, S_DEV), ((0, 16), (1, 16)), -0.2, 0.2), 0.0, 1.0),
        "star_count": draw_star_count(jax.random.fold_in(seeds[7], 71), 0),
    }


DT = 0.3
ALPHA = 0.4
SIGMA = (1.5, 0.5)

def directional(state, axis_dir):
    photons = state[:, 0]
    flux = state[:, 1:4]
    fsq = jnp.minimum(lax.optimization_barrier(jnp.sum(flux * flux, axis=1)) / (photons * photons), 1.0)
    root = jnp.sqrt(4.0 - 3.0 * fsq)
    chi = (3.0 + 4.0 * fsq) / (5.0 + 2.0 * root)
    shape_term = (3.0 / (2.0 + root) + 6.0) / (5.0 + 2.0 * root)
    diag = 0.5 * (1.0 - chi) * photons
    scaled = shape_term / photons
    comps = [flux[:, axis_dir]]
    for other in range(3):
        value = scaled * flux[:, axis_dir] * flux[:, other]
        if other == axis_dir:
            value = value + diag
        comps.append(value)
    return jnp.stack(comps, axis=1)

def transport(state):
    total = jnp.zeros_like(state)
    for axis_dir, axis in ((0, 3), (1, 4), (2, 2)):
        phys = directional(state, axis_dir)
        face = 0.5 * (phys + jnp.roll(phys, -1, axis)) - 0.5 * (jnp.roll(state, -1, axis) - state)
        total = total + face - jnp.roll(face, 1, axis)
    return state - DT * total

def chemistry(state, ion, dens):
    sig = jnp.array(SIGMA, jnp.float32).reshape(2, 1, 1, 1)
    start_n = state[:, 0]
    start_f = state[:, 1:4]
    frac = ion
    for step in range(CHEM_ITERS):
        atten = 1.0 / (1.0 + DT * sig * dens * (1.0 - frac))
        photons = start_n * atten
        gamma = lax.optimization_barrier(jnp.sum(sig * photons, axis=0))
        frac = (ion + DT * gamma) / (1.0 + DT * (gamma + ALPHA * dens * frac))
    return (jnp.concatenate([photons[:, None], start_f * atten[:, None]], axis=1), frac)

def deposit(star_lum, star_cell, star_offset, star_count):
    slots = jnp.arange(S_DEV, dtype=jnp.int32)
    live = (slots[None, None, :] < star_count[:, :, None]).astype(jnp.float32)
    tile_x = jnp.arange(TILES_X, dtype=jnp.int32)[:, None, None]
    tile_y = jnp.arange(TILES_Y, dtype=jnp.int32)[None, :, None]
    cell_x = star_cell[:, :, 0] + tile_x * CX
    cell_y = star_cell[:, :, 1] + tile_y * CY
    cell_z = star_cell[:, :, 2]
    emission = jnp.zeros((G, NZ * NX * NY), jnp.float32)
    for dz in (0, 1):
        for dx in (0, 1):
            for dy in (0, 1):
                wz = star_offset[:, :, 2] if dz else 1.0 - star_offset[:, :, 2]
                wx = star_offset[:, :, 0] if dx else 1.0 - star_offset[:, :, 0]
                wy = star_offset[:, :, 1] if dy else 1.0 - star_offset[:, :, 1]
                weight = wz * wx * wy * live
                index = ((cell_z + dz) % NZ * NX + (cell_x + dx) % NX) * NY + (cell_y + dy) % NY
                values = jnp.moveaxis(star_lum * weight[:, :, None, :], 2, 0).reshape(G, -1)
                emission = emission.at[:, index.reshape(-1)].add(values)
    return emission.reshape(G, NZ, NX, NY)

def reference(radiation, ion_fraction, density, star_lum, star_cell, star_offset, star_count):
    emission = deposit(star_lum, star_cell, star_offset, star_count)
    state = radiation
    ion = ion_fraction
    for step in range(SUBSTEPS):
        state = transport(state)
        state = jnp.concatenate([state[:, :1] + DT * emission[:, None], state[:, 1:]], axis=1)
        state, ion = chemistry(state, ion, density)
    return (state, ion)
```

```python
import functools

import jax
import jax.numpy as jnp
from jax import lax
from jax.experimental import pallas as pl
from jax.experimental.pallas import tpu as pltpu
from jax.sharding import PartitionSpec as P

SUBSTEPS = 4
CHEM_ITERS = 3
DT = 0.3
ALPHA = 0.4
SIGMA = (1.5, 0.5)

MESH = pl.DeviceIdType.MESH
F32 = jnp.float32

ROWS, DEPTH, LANES = 16, 8, 128
HALO = SUBSTEPS
FIELDS = 8
ION, DENS, ARRAYS = 8, 9, 10
STRIP, SLOTS = 24, 5
STRIP_ROW = ROWS + 2 * HALO + 1
TOTAL_ROWS = STRIP_ROW + SLOTS + 1
DIRS = ((1, 1), (1, -1), (-1, 1), (-1, -1), (0, 1), (0, -1), (1, 0), (-1, 0))
SELF_COEF = (1.0 - 3.0 * DT) / (0.5 * DT)


def lane_roll(value, shift):
    if isinstance(shift, int):
        shift = shift % LANES
        return value if shift == 0 else pltpu.roll(value, shift, 1)
    return pltpu.roll(value, lax.rem(shift + LANES, LANES), 1)


def fluxes(u):
    n, fx, fy, fz = u
    n2 = n * n
    f2 = fx * fx + fy * fy + fz * fz
    q = jnp.sqrt(4.0 * n2 - 3.0 * jnp.minimum(f2, n2))
    h = 3.0 / (2.0 * n + q)
    diag = (q - n) * (1.0 / 3.0)
    gx, gy, gz = h * fx, h * fy, h * fz
    pxy, pxz, pyz = gx * fy, gx * fz, gy * fz
    flux_x = (fx, gx * fx + diag, pxy, pxz)
    flux_y = (fy, pxy, gy * fy + diag, pyz)
    flux_z = (fz, pxz, pyz, gz * fz + diag)
    here = []
    for c in range(4):
        side = lane_roll(u[c] - flux_y[c], -1) + lane_roll(u[c] + flux_y[c], 1)
        side = side + pltpu.roll(u[c] - flux_z[c], DEPTH - 1, 0) + pltpu.roll(u[c] + flux_z[c], 1, 0)
        here.append(SELF_COEF * u[c] + side)
    to_lower = [u[c] - flux_x[c] for c in range(4)]
    to_upper = [u[c] + flux_x[c] for c in range(4)]
    return here, to_lower, to_upper


def photochemistry(n1, n2, x0, dens):
    dn = DT * dens
    rec = ALPHA * dn
    m1, m2 = (DT * SIGMA[0]) * n1, (DT * SIGMA[1]) * n2
    x = x0
    for step in range(CHEM_ITERS):
        u = dn * (1.0 - x)
        d1, d2 = 1.0 + SIGMA[0] * u, 1.0 + SIGMA[1] * u
        both = d1 * d2
        gamma = m1 * d2 + m2 * d1
        top = x0 * both + gamma
        bottom = both * (1.0 + rec * x) + gamma
        if step < CHEM_ITERS - 1:
            x = top / bottom
        else:
            inverse = 1.0 / (both * bottom)
            x = top * (both * inverse)
            per_both = bottom * inverse
    return d2 * per_both, d1 * per_both, x


def kernel(
    rad_hbm, ion_hbm, dens_hbm, lum_hbm, cell_hbm, offset_hbm, count_hbm, rad_out, ion_out,
    raw, lum, cell, offset, count, own, own_e, ions, flux_buf, strips, strips_e, final,
    y_send, d_send, ex_send, ey_send, ed_send, x_recv, y_recv, d_recv, ex_recv, ey_recv, ed_recv, raw_out,
    in_sem, out_sem, s_send, s_recv, e_send, e_recv,
):
    nx, ny = lax.axis_size("gx"), lax.axis_size("gy")
    me_x, me_y = lax.axis_index("gx"), lax.axis_index("gy")

    def device(direction):
        dx, dy = direction
        return (lax.rem(me_x + dx + nx, nx), lax.rem(me_y + dy + ny, ny))

    copies_in = [
        pltpu.make_async_copy(src, dst, in_sem.at[i])
        for i, (src, dst) in enumerate(
            (
                (rad_hbm, raw.at[pl.ds(0, FIELDS)]),
                (ion_hbm, raw.at[ION]),
                (dens_hbm, raw.at[DENS]),
                (lum_hbm, lum),
                (cell_hbm, cell),
                (offset_hbm, offset),
                (count_hbm, count),
            )
        )
    ]
    for copy in copies_in:
        copy.start()
    barrier = pltpu.get_barrier_semaphore()
    for direction in DIRS:
        pl.semaphore_signal(barrier, inc=1, device_id=device(direction), device_id_type=MESH)

    lane = lax.broadcasted_iota(jnp.int32, (DEPTH, LANES), 1)
    slot_col = lax.rem(lane, STRIP)
    zeros = jnp.zeros((DEPTH, LANES), F32)

    def between(position, low, width):
        return (position >= low) & (position < low + width)

    def send(src, dst, sems, index, direction):
        copy = pltpu.make_async_remote_copy(
            src_ref=src,
            dst_ref=dst,
            send_sem=sems[0].at[index],
            recv_sem=sems[1].at[index],
            device_id=device(direction),
            device_id_type=MESH,
        )
        copy.start()
        return copy

    for copy in copies_in[:3]:
        copy.wait()

    def unpack(x, packed):
        r = x + HALO
        base = 4 * r + 4 * lax.div(r, SLOTS)
        mask = between(lane, base, 4)
        out = []
        for a in range(ARRAYS):
            row = raw[a, pl.ds(x, DEPTH, stride=ROWS), :]
            own[a, r] = row
            up, down = packed[2 * a], packed[2 * a + 1]
            out.append(jnp.where(mask, lane_roll(row, base + 4), up))
            out.append(jnp.where(mask, lane_roll(row, base), down))
        return tuple(out)

    packed = lax.fori_loop(0, ROWS, unpack, (zeros,) * (2 * ARRAYS))
    for a in range(ARRAYS):
        y_send[0, a] = packed[2 * a]
        y_send[1, a] = packed[2 * a + 1]

    def to_upper_corner(value, first):
        low = lane_roll(value, 24 * first - 76)
        return low

    def corner(value, dx, place, last_row):
        at = STRIP * place
        if dx > 0:
            out = jnp.where(between(lane, at, 16), lane_roll(value, at - 76), 0.0)
            if last_row:
                out = jnp.where(between(lane, at + 16, 4), lane_roll(value, at - 80), out)
            return out
        out = jnp.where(between(lane, at, 4), lane_roll(value, at - 16), 0.0)
        return jnp.where(between(lane, at + 4, 12), lane_roll(value, at - 20), out)

    for i, (dx, dy) in enumerate(DIRS[:4]):
        side = 0 if dy > 0 else 1
        for part in range(2):
            total = zeros
            for place in range(SLOTS):
                total = total + corner(packed[2 * (SLOTS * part + place) + side], dx, place, False)
            d_send[i, part] = total

    pl.semaphore_wait(barrier, len(DIRS))
    state_sems, emit_sems = (s_send, s_recv), (e_send, e_recv)
    state_copies = []
    for i, direction in enumerate(DIRS[:4]):
        state_copies.append(send(d_send.at[i], d_recv.at[i], state_sems, i, direction))
    for i, direction in enumerate(DIRS[4:6]):
        state_copies.append(send(y_send.at[i], y_recv.at[i], state_sems, 4 + i, direction))
    for i, direction in enumerate(DIRS[6:]):
        first = ROWS if i == 0 else HALO
        rows = own.at[:, pl.ds(first, HALO)]
        state_copies.append(send(rows, x_recv.at[i], state_sems, 6 + i, direction))

    for copy in copies_in[3:]:
        copy.wait()
    stars = lum.shape[1]
    live = (lax.broadcasted_iota(jnp.int32, (1, stars), 1) < count[...]).astype(F32)

    def corner_weight(axis, position, upper=None):
        low = cell[axis : axis + 1, :]
        frac = offset[axis : axis + 1, :]
        high = low + 1 if upper is None else upper(low + 1)
        return jnp.where(low == position, 1.0 - frac, 0.0) + jnp.where(high == position, frac, 0.0)

    z_at = lax.broadcasted_iota(jnp.int32, (DEPTH, stars), 0)
    weight_z = corner_weight(2, z_at, lambda c: jnp.where(c >= DEPTH, c - DEPTH, c))
    strength = [weight_z * (lum[g : g + 1, :] * live * DT) for g in range(2)]
    y_at = lax.broadcasted_iota(jnp.int32, (LANES, stars), 0)
    weight_y = corner_weight(1, y_at)
    weight_x = corner_weight(0, y_at)
    over_y = corner_weight(1, jnp.full((1, stars), LANES, jnp.int32))
    spread = []
    for g in range(2):
        for x in range(ROWS + 1):
            spread.append(strength[g] * corner_weight(0, jnp.full((1, stars), x, jnp.int32)))
    contract = functools.partial(
        lax.dot_general,
        dimension_numbers=(((1,), (1,)), ((), ())),
        precision=lax.Precision.HIGHEST,
        preferred_element_type=F32,
    )
    deposit = contract(jnp.concatenate(spread, axis=0), weight_y)
    column = contract(jnp.concatenate([s * over_y for s in strength], axis=0), weight_x)
    for g in range(2):
        for x in range(ROWS + 1):
            at = (g * (ROWS + 1) + x) * DEPTH
            own_e[g, HALO + x] = deposit[at : at + DEPTH]
    for v in range(SLOTS):
        for g in range(2):
            strips_e[g, v] = zeros

    def pack_e(x, carry):
        r = x + HALO
        s = lax.div(r, SLOTS)
        v = r - SLOTS * s
        base = 4 * r + 4 * s
        at = STRIP * s
        mask = between(lane, base, 4)
        out = []
        for g in range(2):
            row = own_e[g, r]
            over = lane_roll(column[g * DEPTH : (g + 1) * DEPTH], LANES - 1 - x)
            moved = jnp.where(lane == LANES - 1, over, lane_roll(row, -1))
            out.append(jnp.where(mask, lane_roll(moved, base + 4), carry[2 * g]))
            out.append(jnp.where(mask, lane_roll(row, base), carry[2 * g + 1]))
            strip = strips_e[g, v]
            strip = jnp.where(between(lane, at + 1, 8), lane_roll(moved, at + 9), strip)
            strips_e[g, v] = jnp.where(between(lane, at + 16, 8), lane_roll(row, at + 16), strip)
        return tuple(out)

    packed_e = lax.fori_loop(0, ROWS + 1, pack_e, (zeros,) * 4)
    for g in range(2):
        ey_send[0, g] = packed_e[2 * g]
        ey_send[1, g] = packed_e[2 * g + 1]
    for i, (dx, dy) in enumerate(DIRS[:4]):
        side = 0 if dy > 0 else 1
        ed_send[i] = corner(packed_e[side], dx, 0, True) + corner(packed_e[2 + side], dx, 1, True)
    for g in range(2):
        for i, (first, moved) in enumerate(((ROWS + 1, 1), (HALO, ROWS + HALO))):
            total = zeros
            for j in range(HALO):
                ex_send[i, g, j] = own_e[g, first + j]
                s, v = divmod(first + j, SLOTS)
                place = (moved + j) % SLOTS
                piece = lane_roll(strips_e[g, v], STRIP * (place - s))
                total = jnp.where(between(lane, STRIP * place, STRIP), piece, total)
            ex_send[i, g, HALO] = total
    emit_copies = []
    for i, direction in enumerate(DIRS[:4]):
        emit_copies.append(send(ed_send.at[i], ed_recv.at[i], emit_sems, i, direction))
    for i, direction in enumerate(DIRS[4:6]):
        emit_copies.append(send(ey_send.at[i], ey_recv.at[i], emit_sems, 4 + i, direction))
    for i, direction in enumerate(DIRS[6:]):
        emit_copies.append(send(ex_send.at[i], ex_recv.at[i], emit_sems, 6 + i, direction))

    def store_flux(k, g, r, u):
        here, to_lower, to_upper = fluxes(u)
        for c in range(4):
            flux_buf[k, g, c, r] = here[c]
            flux_buf[k, g, 4 + c, r] = to_lower[c]
            flux_buf[k, g, 8 + c, r] = to_upper[c]

    def substep(k, r):
        u = []
        for g in range(2):
            for c in range(4):
                total = flux_buf[k - 1, g, c, r] + (flux_buf[k - 1, g, 4 + c, r + 1] + flux_buf[k - 1, g, 8 + c, r - 1])
                u.append((0.5 * DT) * total)
            u[4 * g] = u[4 * g] + own_e[g, r]
        att1, att2, x = photochemistry(u[0], u[4], ions[k - 1, r], ions[SUBSTEPS, r])
        u = [value * (att1 if i < 4 else att2) for i, value in enumerate(u)]
        if k < SUBSTEPS:
            store_flux(k, 0, r, u[:4])
            store_flux(k, 1, r, u[4:])
            ions[k, r] = x
        else:
            for i in range(FIELDS):
                final[i, r] = u[i]
            final[ION, r] = x

    def start_row(i, carry):
        r = HALO + i
        ions[0, r] = own[ION, r]
        ions[SUBSTEPS, r] = own[DENS, r]
        for g in range(2):
            store_flux(0, g, r, [own[4 * g + c, r] for c in range(4)])
        return carry

    lax.fori_loop(0, ROWS, start_row, 0)
    for k in range(1, SUBSTEPS + 1):

        def inner(i, carry, k=k):
            substep(k, HALO + k + 2 * i)
            substep(k, HALO + k + 2 * i + 1)
            return carry

        lax.fori_loop(0, (ROWS - 2 * k) // 2, inner, 0)

    def pack_strip(row, s, old):
        at = STRIP * s
        new = jnp.where(between(lane, at, 8), lane_roll(row, at + 8), old)
        return jnp.where(between(lane, at + 16, 8), lane_roll(row, at + 16), new)

    for a in range(ARRAYS):
        for v in range(SLOTS):
            strips[a, v] = zeros

    def own_strip(i, carry):
        r = HALO + i
        s = lax.div(r, SLOTS)
        v = r - SLOTS * s
        for a in range(ARRAYS):
            strips[a, v] = pack_strip(own[a, r], s, strips[a, v])
        return carry

    lax.fori_loop(0, ROWS, own_strip, 0)

    for i in (6, 7):
        state_copies[i].wait_recv()
        emit_copies[i].wait_recv()

    def start_edge(j, carry):
        for i, r in ((0, j), (1, ROWS + HALO + j)):
            ions[0, r] = x_recv[i, ION, j]
            ions[SUBSTEPS, r] = x_recv[i, DENS, j]
            for g in range(2):
                store_flux(0, g, r, [x_recv[i, 4 * g + c, j] for c in range(4)])
        return carry

    lax.fori_loop(0, HALO, start_edge, 0)
    for g in range(2):
        for j in range(HALO):
            low, high = 1 + j, ROWS + HALO + j
            if j < HALO - 1:
                own_e[g, low] = ex_recv[0, g, j]
            else:
                own_e[g, low] = own_e[g, low] + ex_recv[0, g, j]
            if j == 0:
                own_e[g, high] = own_e[g, high] + ex_recv[1, g, j]
            else:
                own_e[g, high] = ex_recv[1, g, j]
    for k in range(1, SUBSTEPS + 1):

        def edge(i, carry, k=k):
            substep(k, k + i)
            substep(k, ROWS + HALO - k + i)
            return carry

        lax.fori_loop(0, HALO, edge, 0)

    for i in range(6):
        state_copies[i].wait_recv()
        emit_copies[i].wait_recv()

    def unslot(value, place, slot, width):
        return jnp.where(between(lane, STRIP * slot, width), lane_roll(value, STRIP * (slot - place)), 0.0)

    for a in range(ARRAYS):
        part, place = divmod(a, SLOTS)
        edges = []
        for side in range(2):
            edge_cols = y_recv[side, a]
            edge_cols = edge_cols + unslot(d_recv[side, part], place, 0, 16)
            edge_cols = edge_cols + unslot(d_recv[2 + side, part], place, 4, 16)
            edges.append(edge_cols)
        for v in range(SLOTS):
            value = strips[a, v]
            if v < HALO:
                value = pack_strip(x_recv[0, a, v], 0, value)
                value = pack_strip(x_recv[1, a, v], SLOTS - 1, value)
            value = jnp.where(between(slot_col, 12, 4), lane_roll(edges[0], 12 - 4 * v), value)
            value = jnp.where(between(slot_col, 8, 4), lane_roll(edges[1], 8 - 4 * v), value)
            strips[a, v] = value
    for g in range(2):
        edges = []
        for side in range(2):
            edge_cols = ey_recv[side, g]
            edge_cols = edge_cols + unslot(ed_recv[side], g, 0, 20)
            edge_cols = edge_cols + unslot(ed_recv[2 + side], g, 4, 20)
            edges.append(edge_cols)
        for v in range(SLOTS):
            value = strips_e[g, v]
            value = value + jnp.where(between(lane, 0, STRIP), lane_roll(ex_recv[0, g, HALO], -STRIP * v), 0.0)
            value = value + jnp.where(
                between(lane, STRIP * (SLOTS - 1), STRIP),
                lane_roll(ex_recv[1, g, HALO], STRIP * (SLOTS - 1 - v)),
                0.0,
            )
            value = value + jnp.where(between(slot_col, 13, 4), lane_roll(edges[0], 13 - 4 * v), 0.0)
            value = value + jnp.where(between(slot_col, 8, 4), lane_roll(edges[1], 8 - 4 * v), 0.0)
            own_e[g, STRIP_ROW + v] = value

    def wrap_strips(k):
        for g in range(2):
            for c in range(4):
                flux_buf[k, g, 4 + c, STRIP_ROW + SLOTS] = lane_roll(flux_buf[k, g, 4 + c, STRIP_ROW], -STRIP)
                flux_buf[k, g, 8 + c, STRIP_ROW - 1] = lane_roll(flux_buf[k, g, 8 + c, STRIP_ROW + SLOTS - 1], STRIP)

    def start_strip(v, carry):
        ions[0, STRIP_ROW + v] = strips[ION, v]
        ions[SUBSTEPS, STRIP_ROW + v] = strips[DENS, v]
        for g in range(2):
            store_flux(0, g, STRIP_ROW + v, [strips[4 * g + c, v] for c in range(4)])
        return carry

    lax.fori_loop(0, SLOTS, start_strip, 0)
    for k in range(1, SUBSTEPS + 1):
        wrap_strips(k - 1)

        def strip(v, carry, k=k):
            substep(k, STRIP_ROW + v)
            return carry

        lax.fori_loop(0, SLOTS, strip, 0)

    def merge(x, carry):
        r = HALO + x
        s = lax.div(r, SLOTS)
        v = r - SLOTS * s
        for a in range(FIELDS + 1):
            edge_cols = final[a, STRIP_ROW + v]
            value = final[a, r]
            value = jnp.where(lane < HALO, lane_roll(edge_cols, LANES - 16 - STRIP * s), value)
            value = jnp.where(lane >= LANES - HALO, lane_roll(edge_cols, LANES - 8 - STRIP * s), value)
            raw_out[a, pl.ds(x, DEPTH, stride=ROWS), :] = value
        return carry

    lax.fori_loop(0, ROWS, merge, 0)
    copies_out = [
        pltpu.make_async_copy(raw_out.at[pl.ds(0, FIELDS)], rad_out, out_sem.at[0]),
        pltpu.make_async_copy(raw_out.at[ION], ion_out, out_sem.at[1]),
    ]
    for copy in copies_out:
        copy.start()
    for copy in state_copies + emit_copies:
        copy.wait_send()
    for copy in copies_out:
        copy.wait()


def on_device(radiation, ion_fraction, density, star_lum, star_cell, star_offset, star_count):
    groups, comps, depth, rows, lanes = radiation.shape
    assert (groups * comps, depth, rows, lanes) == (FIELDS, DEPTH, ROWS, LANES)
    stars = star_lum.shape[3]
    plane = (depth * rows, lanes)
    vmem = lambda *shape: pltpu.VMEM(shape + (DEPTH, LANES), F32)
    anywhere = pl.BlockSpec(memory_space=pl.ANY)
    rad, ion = pl.pallas_call(
        kernel,
        out_shape=(
            jax.ShapeDtypeStruct((FIELDS,) + plane, F32),
            jax.ShapeDtypeStruct(plane, F32),
        ),
        in_specs=[anywhere] * 7,
        out_specs=(anywhere, anywhere),
        scratch_shapes=[
            pltpu.VMEM((ARRAYS,) + plane, F32),
            pltpu.VMEM((2, stars), F32),
            pltpu.VMEM((3, stars), jnp.int32),
            pltpu.VMEM((3, stars), F32),
            pltpu.VMEM((1, 1), jnp.int32),
            vmem(ARRAYS, ROWS + 2 * HALO),
            vmem(2, TOTAL_ROWS),
            vmem(SUBSTEPS + 1, TOTAL_ROWS),
            vmem(SUBSTEPS, 2, 12, TOTAL_ROWS),
            vmem(ARRAYS, SLOTS),
            vmem(2, SLOTS),
            vmem(FIELDS + 1, TOTAL_ROWS),
            vmem(2, ARRAYS),
            vmem(4, 2),
            vmem(2, 2, HALO + 1),
            vmem(2, 2),
            vmem(4),
            vmem(2, ARRAYS, HALO),
            vmem(2, ARRAYS),
            vmem(4, 2),
            vmem(2, 2, HALO + 1),
            vmem(2, 2),
            vmem(4),
            pltpu.VMEM((FIELDS + 1,) + plane, F32),
            pltpu.SemaphoreType.DMA((7,)),
            pltpu.SemaphoreType.DMA((2,)),
            pltpu.SemaphoreType.DMA((8,)),
            pltpu.SemaphoreType.DMA((8,)),
            pltpu.SemaphoreType.DMA((8,)),
            pltpu.SemaphoreType.DMA((8,)),
        ],
        compiler_params=pltpu.CompilerParams(
            collective_id=0, has_side_effects=True, vmem_limit_bytes=40 * 1024 * 1024
        ),
    )(
        radiation.reshape((FIELDS,) + plane),
        ion_fraction.reshape(plane),
        density.reshape(plane),
        star_lum[0, 0],
        star_cell[0, 0],
        star_offset[0, 0],
        star_count,
    )
    return rad.reshape(radiation.shape), ion.reshape(ion_fraction.shape)


def solution(mesh):
    return jax.shard_map(
        on_device,
        mesh=mesh,
        in_specs=(
            P(None, None, None, "gx", "gy"),
            P(None, "gx", "gy"),
            P(None, "gx", "gy"),
            P("gx", "gy", None, None),
            P("gx", "gy", None, None),
            P("gx", "gy", None, None),
            P("gx", "gy"),
        ),
        out_specs=(P(None, None, None, "gx", "gy"), P(None, "gx", "gy")),
        check_vma=False,
    )
```

```python
import functools

import jax
import jax.numpy as jnp
from jax import lax
from jax.experimental import pallas as pl
from jax.experimental.pallas import tpu as pltpu
from jax.sharding import PartitionSpec as P

SUBSTEPS = 4
CHEM_ITERS = 3
DT = 0.3
ALPHA = 0.4
SIGMA = (1.5, 0.5)

MESH = pl.DeviceIdType.MESH
F32 = jnp.float32

ROWS, DEPTH, LANES = 16, 8, 128
HALO = SUBSTEPS
FIELDS = 8
ION, DENS, STATE = 8, 9, 10
ARRAYS = STATE + 2
STRIP, SLOTS = 24, 5
STRIP_ROW = ROWS + 2 * HALO + 1
TOTAL_ROWS = STRIP_ROW + SLOTS + 1
DIRS = ((1, 1), (1, -1), (-1, 1), (-1, -1), (0, 1), (0, -1), (1, 0), (-1, 0))
SELF_COEF = (1.0 - 3.0 * DT) / (0.5 * DT)


def lane_roll(value, shift):
    if isinstance(shift, int):
        shift = shift % LANES
        return value if shift == 0 else pltpu.roll(value, shift, 1)
    return pltpu.roll(value, lax.rem(shift + LANES, LANES), 1)


def fluxes(u):
    n, fx, fy, fz = u
    n2 = n * n
    f2 = fx * fx + fy * fy + fz * fz
    q = jnp.sqrt(4.0 * n2 - 3.0 * jnp.minimum(f2, n2))
    h = 3.0 / (2.0 * n + q)
    diag = (q - n) * (1.0 / 3.0)
    gx, gy, gz = h * fx, h * fy, h * fz
    pxy, pxz, pyz = gx * fy, gx * fz, gy * fz
    flux_x = (fx, gx * fx + diag, pxy, pxz)
    flux_y = (fy, pxy, gy * fy + diag, pyz)
    flux_z = (fz, pxz, pyz, gz * fz + diag)
    here = []
    for c in range(4):
        side = lane_roll(u[c] - flux_y[c], -1) + lane_roll(u[c] + flux_y[c], 1)
        side = side + pltpu.roll(u[c] - flux_z[c], DEPTH - 1, 0) + pltpu.roll(u[c] + flux_z[c], 1, 0)
        here.append(SELF_COEF * u[c] + side)
    to_lower = [u[c] - flux_x[c] for c in range(4)]
    to_upper = [u[c] + flux_x[c] for c in range(4)]
    return here, to_lower, to_upper


def photochemistry(n1, n2, x0, dens):
    dn = DT * dens
    rec = ALPHA * dn
    m1, m2 = (DT * SIGMA[0]) * n1, (DT * SIGMA[1]) * n2
    x = x0
    for step in range(CHEM_ITERS):
        u = dn * (1.0 - x)
        d1, d2 = 1.0 + SIGMA[0] * u, 1.0 + SIGMA[1] * u
        both = d1 * d2
        gamma = m1 * d2 + m2 * d1
        top = x0 * both + gamma
        bottom = both * (1.0 + rec * x) + gamma
        if step < CHEM_ITERS - 1:
            x = top / bottom
        else:
            inverse = 1.0 / (both * bottom)
            x = top * (both * inverse)
            per_both = bottom * inverse
    return d2 * per_both, d1 * per_both, x


def kernel(
    rad_hbm, ion_hbm, dens_hbm, lum_hbm, cell_hbm, offset_hbm, count_hbm, rad_out, ion_out,
    raw, lum, cell, offset, count, own, own_e, ions, flux_buf, strips, final,
    y_send, d_send, e_send, x_recv, y_recv, d_recv, e_recv, in_sem, send_sem, recv_sem,
):
    nx, ny = lax.axis_size("gx"), lax.axis_size("gy")
    me_x, me_y = lax.axis_index("gx"), lax.axis_index("gy")

    def device(direction):
        dx, dy = direction
        return (lax.rem(me_x + dx + nx, nx), lax.rem(me_y + dy + ny, ny))

    copies_in = [
        pltpu.make_async_copy(src, dst, in_sem.at[i])
        for i, (src, dst) in enumerate(
            (
                (rad_hbm, raw.at[pl.ds(0, FIELDS)]),
                (ion_hbm, raw.at[ION]),
                (dens_hbm, raw.at[DENS]),
                (lum_hbm, lum),
                (cell_hbm, cell),
                (offset_hbm, offset),
                (count_hbm, count),
            )
        )
    ]
    for copy in copies_in:
        copy.start()
    barrier = pltpu.get_barrier_semaphore()
    for direction in DIRS:
        pl.semaphore_signal(barrier, inc=1, device_id=device(direction), device_id_type=MESH)

    lane = lax.broadcasted_iota(jnp.int32, (DEPTH, LANES), 1)
    slot_col = lax.rem(lane, STRIP)
    zeros = jnp.zeros((DEPTH, LANES), F32)

    def between(position, low, width):
        return (position >= low) & (position < low + width)

    def send(src, dst, index, direction):
        copy = pltpu.make_async_remote_copy(
            src_ref=src,
            dst_ref=dst,
            send_sem=send_sem.at[index],
            recv_sem=recv_sem.at[index],
            device_id=device(direction),
            device_id_type=MESH,
        )
        copy.start()
        return copy

    for copy in copies_in[:3]:
        copy.wait()

    def unpack(x, carry):
        for a in range(STATE):
            own[a, x + HALO] = raw[a, pl.ds(x, DEPTH, stride=ROWS), :]
        return carry

    lax.fori_loop(0, ROWS, unpack, 0)

    for copy in copies_in[3:]:
        copy.wait()
    stars = lum.shape[1]
    live = (lax.broadcasted_iota(jnp.int32, (1, stars), 1) < count[...]).astype(F32)

    def corner_weight(axis, position, wrapped=False):
        low, frac = cell[axis], offset[axis]
        high = low + 1
        if wrapped:
            high = jnp.where(high >= DEPTH, high - DEPTH, high)
        return jnp.where(low == position, 1.0 - frac, 0.0) + jnp.where(high == position, frac, 0.0)

    z_at = lax.broadcasted_iota(jnp.int32, (DEPTH, stars), 0)
    weight_z = corner_weight(2, z_at, True)
    strength = [weight_z * (lum[g : g + 1, :] * live * DT) for g in range(2)]
    y_at = lax.broadcasted_iota(jnp.int32, (LANES, stars), 0)
    weight_y = corner_weight(1, y_at)
    weight_x = corner_weight(0, y_at)
    over_y = corner_weight(1, jnp.full((1, stars), LANES, jnp.int32))
    weight_rows = [corner_weight(0, jnp.full((1, stars), x, jnp.int32)) for x in range(ROWS + 1)]
    spread = [strength[g] * weight_rows[x] for g in range(2) for x in range(ROWS + 1)]
    contract = functools.partial(
        lax.dot_general,
        dimension_numbers=(((1,), (1,)), ((), ())),
        precision=lax.Precision.HIGHEST,
        preferred_element_type=F32,
    )
    deposit = contract(jnp.concatenate(spread, axis=0), weight_y)
    column = contract(jnp.concatenate([s * over_y for s in strength], axis=0), weight_x)
    moved = [[None] * (ROWS + 1) for _ in range(2)]
    for g in range(2):
        for x in range(ROWS + 1):
            at = (g * (ROWS + 1) + x) * DEPTH
            row = deposit[at : at + DEPTH]
            own_e[g, HALO + x] = row
            over = lane_roll(column[g * DEPTH : (g + 1) * DEPTH], LANES - 1 - x)
            moved[g][x] = jnp.where(lane == LANES - 1, over, lane_roll(row, -1))

    def array_row(a, r):
        return own[a, r] if a < STATE else own_e[a - STATE, r]

    packed = {}
    for a in range(ARRAYS):
        for side in range(2):
            total = zeros
            for x in range(ROWS + (a >= STATE)):
                base = 4 * (x + HALO) + 4 * ((x + HALO) // SLOTS)
                if side == 1:
                    piece = lane_roll(array_row(a, x + HALO), base)
                else:
                    row = array_row(a, x + HALO) if a < STATE else moved[a - STATE][x]
                    piece = lane_roll(row, base + 4)
                total = jnp.where(between(lane, base, 4), piece, total)
            packed[a, side] = total
            y_send[side, a] = total

    def corner(value, dx, place, last_row):
        at = STRIP * place
        if dx > 0:
            out = jnp.where(between(lane, at, 16), lane_roll(value, at - 76), 0.0)
            if last_row:
                out = jnp.where(between(lane, at + 16, 4), lane_roll(value, at - 80), out)
            return out
        out = jnp.where(between(lane, at, 4), lane_roll(value, at - 16), 0.0)
        return jnp.where(between(lane, at + 4, 12), lane_roll(value, at - 20), out)

    for i, (dx, dy) in enumerate(DIRS[:4]):
        side = 0 if dy > 0 else 1
        for part in range(3):
            total = zeros
            for place in range(min(SLOTS, ARRAYS - SLOTS * part)):
                a = SLOTS * part + place
                total = total + corner(packed[a, side], dx, place, a >= STATE)
            d_send[i, part] = total

    for g in range(2):
        strip = []
        for v in range(SLOTS):
            total = zeros
            for s in range(SLOTS):
                x, at = SLOTS * s + v - HALO, STRIP * s
                if 0 <= x <= ROWS:
                    total = jnp.where(between(lane, at + 1, 8), lane_roll(moved[g][x], at + 9), total)
                    total = jnp.where(between(lane, at + 16, 8), lane_roll(own_e[g, x + HALO], at + 16), total)
            strip.append(total)
            strips[STATE + g, v] = total
        for i, (first, target) in enumerate(((ROWS + 1, 1), (HALO, ROWS + HALO))):
            total = zeros
            for j in range(HALO):
                e_send[i, g, j] = own_e[g, first + j]
                s, v = divmod(first + j, SLOTS)
                place = (target + j) % SLOTS
                piece = lane_roll(strip[v], STRIP * (place - s))
                total = jnp.where(between(lane, STRIP * place, STRIP), piece, total)
            e_send[i, g, HALO] = total

    pl.semaphore_wait(barrier, len(DIRS))
    copies = []
    for i, direction in enumerate(DIRS[:4]):
        copies.append(send(d_send.at[i], d_recv.at[i], i, direction))
    for i, direction in enumerate(DIRS[4:6]):
        copies.append(send(y_send.at[i], y_recv.at[i], 4 + i, direction))
    for i, direction in enumerate(DIRS[6:]):
        rows = own.at[:, pl.ds(ROWS if i == 0 else HALO, HALO)]
        copies.append(send(rows, x_recv.at[i], 6 + i, direction))
        copies.append(send(e_send.at[i], e_recv.at[i], 8 + i, direction))

    def store_flux(k, g, r, u):
        here, to_lower, to_upper = fluxes(u)
        for c in range(4):
            flux_buf[k, g, c, r] = here[c]
            flux_buf[k, g, 4 + c, r] = to_lower[c]
            flux_buf[k, g, 8 + c, r] = to_upper[c]

    def substep(k, r):
        u = []
        for g in range(2):
            for c in range(4):
                total = flux_buf[k - 1, g, c, r] + (flux_buf[k - 1, g, 4 + c, r + 1] + flux_buf[k - 1, g, 8 + c, r - 1])
                u.append((0.5 * DT) * total)
            u[4 * g] = u[4 * g] + own_e[g, r]
        att1, att2, x = photochemistry(u[0], u[4], ions[k - 1, r], ions[SUBSTEPS, r])
        u = [value * (att1 if i < 4 else att2) for i, value in enumerate(u)]
        if k < SUBSTEPS:
            store_flux(k, 0, r, u[:4])
            store_flux(k, 1, r, u[4:])
            ions[k, r] = x
        else:
            for i in range(FIELDS):
                final[i, r] = u[i]
            final[ION, r] = x

    def start_row(i, carry):
        r = HALO + i
        ions[0, r] = own[ION, r]
        ions[SUBSTEPS, r] = own[DENS, r]
        for g in range(2):
            store_flux(0, g, r, [own[4 * g + c, r] for c in range(4)])
        return carry

    lax.fori_loop(0, ROWS, start_row, 0)
    for k in range(1, SUBSTEPS + 1):

        def inner(i, carry, k=k):
            substep(k, HALO + k + 2 * i)
            substep(k, HALO + k + 2 * i + 1)
            return carry

        lax.fori_loop(0, (ROWS - 2 * k) // 2, inner, 0)

    def pack_strip(row, s, old):
        at = STRIP * s
        new = jnp.where(between(lane, at, 8), lane_roll(row, at + 8), old)
        return jnp.where(between(lane, at + 16, 8), lane_roll(row, at + 16), new)

    for a in range(STATE):
        for v in range(SLOTS):
            total = zeros
            for s in range(SLOTS):
                if HALO <= SLOTS * s + v < HALO + ROWS:
                    total = pack_strip(own[a, SLOTS * s + v], s, total)
            strips[a, v] = total

    for copy in copies[6:]:
        copy.wait_recv()

    def start_edge(j, carry):
        for i, r in ((0, j), (1, ROWS + HALO + j)):
            ions[0, r] = x_recv[i, ION, j]
            ions[SUBSTEPS, r] = x_recv[i, DENS, j]
            for g in range(2):
                store_flux(0, g, r, [x_recv[i, 4 * g + c, j] for c in range(4)])
        return carry

    lax.fori_loop(0, HALO, start_edge, 0)
    for g in range(2):
        for j in range(HALO):
            low, high = 1 + j, ROWS + HALO + j
            if j < HALO - 1:
                own_e[g, low] = e_recv[0, g, j]
            else:
                own_e[g, low] = own_e[g, low] + e_recv[0, g, j]
            if j == 0:
                own_e[g, high] = own_e[g, high] + e_recv[1, g, j]
            else:
                own_e[g, high] = e_recv[1, g, j]
    for k in range(1, SUBSTEPS + 1):

        def edge(i, carry, k=k):
            substep(k, k + i)
            substep(k, ROWS + HALO - k + i)
            return carry

        lax.fori_loop(0, HALO, edge, 0)

    for copy in copies[:6]:
        copy.wait_recv()

    def unslot(value, place, slot, width):
        return jnp.where(between(lane, STRIP * slot, width), lane_roll(value, STRIP * (slot - place)), 0.0)

    for a in range(ARRAYS):
        part, place = divmod(a, SLOTS)
        deposits = a >= STATE
        edges = []
        for side in range(2):
            edge_cols = y_recv[side, a]
            edge_cols = edge_cols + unslot(d_recv[side, part], place, 0, 20 if deposits else 16)
            edge_cols = edge_cols + unslot(d_recv[2 + side, part], place, 4, 16)
            edges.append(edge_cols)
        for v in range(SLOTS):
            value = strips[a, v]
            if deposits:
                g = a - STATE
                last = STRIP * (SLOTS - 1)
                lower, upper = e_recv[0, g, HALO], e_recv[1, g, HALO]
                value = value + jnp.where(lane < STRIP, lane_roll(lower, -STRIP * v), 0.0)
                value = value + jnp.where(between(lane, last, STRIP), lane_roll(upper, last - STRIP * v), 0.0)
                value = value + jnp.where(between(slot_col, 13, 4), lane_roll(edges[0], 13 - 4 * v), 0.0)
                value = value + jnp.where(between(slot_col, 8, 4), lane_roll(edges[1], 8 - 4 * v), 0.0)
                own_e[g, STRIP_ROW + v] = value
                continue
            if v < HALO:
                value = pack_strip(x_recv[0, a, v], 0, value)
                value = pack_strip(x_recv[1, a, v], SLOTS - 1, value)
            value = jnp.where(between(slot_col, 12, 4), lane_roll(edges[0], 12 - 4 * v), value)
            value = jnp.where(between(slot_col, 8, 4), lane_roll(edges[1], 8 - 4 * v), value)
            strips[a, v] = value

    def wrap_strips(k):
        for g in range(2):
            for c in range(4):
                flux_buf[k, g, 4 + c, STRIP_ROW + SLOTS] = lane_roll(flux_buf[k, g, 4 + c, STRIP_ROW], -STRIP)
                flux_buf[k, g, 8 + c, STRIP_ROW - 1] = lane_roll(flux_buf[k, g, 8 + c, STRIP_ROW + SLOTS - 1], STRIP)

    def start_strip(v, carry):
        ions[0, STRIP_ROW + v] = strips[ION, v]
        ions[SUBSTEPS, STRIP_ROW + v] = strips[DENS, v]
        for g in range(2):
            store_flux(0, g, STRIP_ROW + v, [strips[4 * g + c, v] for c in range(4)])
        return carry

    lax.fori_loop(0, SLOTS, start_strip, 0)
    for k in range(1, SUBSTEPS + 1):
        wrap_strips(k - 1)

        for v in range(SLOTS):
            substep(k, STRIP_ROW + v)

    for x in range(ROWS):
        s, v = divmod(x + HALO, SLOTS)
        for a in range(FIELDS + 1):
            edge_cols = final[a, STRIP_ROW + v]
            value = final[a, x + HALO]
            value = jnp.where(lane < HALO, lane_roll(edge_cols, -16 - STRIP * s), value)
            value = jnp.where(lane >= LANES - HALO, lane_roll(edge_cols, -8 - STRIP * s), value)
            if a < FIELDS:
                rad_out[a, pl.ds(x, DEPTH, stride=ROWS), :] = value
            else:
                ion_out[pl.ds(x, DEPTH, stride=ROWS), :] = value
    for copy in copies:
        copy.wait_send()


def on_device(radiation, ion_fraction, density, star_lum, star_cell, star_offset, star_count):
    groups, comps, depth, rows, lanes = radiation.shape
    assert (groups * comps, depth, rows, lanes) == (FIELDS, DEPTH, ROWS, LANES)
    stars = star_lum.shape[3]
    plane = (depth * rows, lanes)
    vmem = lambda *shape: pltpu.VMEM(shape + (DEPTH, LANES), F32)
    hbm = lambda value: pltpu.with_memory_space_constraint(value, pltpu.HBM)
    rad, ion = pl.pallas_call(
        kernel,
        out_shape=(
            jax.ShapeDtypeStruct((FIELDS,) + plane, F32),
            jax.ShapeDtypeStruct(plane, F32),
        ),
        in_specs=[pl.BlockSpec(memory_space=pltpu.HBM)] * 7,
        out_specs=(pl.BlockSpec(memory_space=pltpu.VMEM),) * 2,
        scratch_shapes=[
            pltpu.VMEM((STATE,) + plane, F32),
            pltpu.VMEM((2, stars), F32),
            pltpu.VMEM((3, 1, stars), jnp.int32),
            pltpu.VMEM((3, 1, stars), F32),
            pltpu.VMEM((1, 1), jnp.int32),
            vmem(STATE, ROWS + 2 * HALO),
            vmem(2, TOTAL_ROWS),
            vmem(SUBSTEPS + 1, TOTAL_ROWS),
            vmem(SUBSTEPS, 2, 12, TOTAL_ROWS),
            vmem(ARRAYS, SLOTS),
            vmem(FIELDS + 1, TOTAL_ROWS),
            vmem(2, ARRAYS),
            vmem(4, 3),
            vmem(2, 2, HALO + 1),
            vmem(2, STATE, HALO),
            vmem(2, ARRAYS),
            vmem(4, 3),
            vmem(2, 2, HALO + 1),
            pltpu.SemaphoreType.DMA((7,)),
            pltpu.SemaphoreType.DMA((10,)),
            pltpu.SemaphoreType.DMA((10,)),
        ],
        compiler_params=pltpu.CompilerParams(
            collective_id=0, has_side_effects=True, vmem_limit_bytes=40 * 1024 * 1024
        ),
    )(
        hbm(radiation.reshape((FIELDS,) + plane)),
        hbm(ion_fraction.reshape(plane)),
        hbm(density.reshape(plane)),
        hbm(star_lum[0, 0]),
        hbm(star_cell.reshape(3, 1, stars)),
        hbm(star_offset.reshape(3, 1, stars)),
        star_count,
    )
    return rad.reshape(radiation.shape), ion.reshape(ion_fraction.shape)


def solution(mesh):
    return jax.shard_map(
        on_device,
        mesh=mesh,
        in_specs=(
            P(None, None, None, "gx", "gy"),
            P(None, "gx", "gy"),
            P(None, "gx", "gy"),
            P("gx", "gy", None, None),
            P("gx", "gy", None, None),
            P("gx", "gy", None, None),
            P("gx", "gy"),
        ),
        out_specs=(P(None, None, None, "gx", "gy"), P(None, "gx", "gy")),
        check_vma=False,
    )
```

```python
import functools

import jax
import jax.numpy as jnp
from jax import lax
from jax.experimental import pallas as pl
from jax.experimental.pallas import tpu as pltpu
from jax.sharding import PartitionSpec as P

SUBSTEPS = 4
CHEM_ITERS = 3
DT = 0.3
ALPHA = 0.4
SIGMA = (1.5, 0.5)

MESH = pl.DeviceIdType.MESH
F32 = jnp.float32

ROWS, DEPTH, LANES = 16, 8, 128
HALO = SUBSTEPS
FIELDS = 8
ION, DENS, STATE = 8, 9, 10
ARRAYS = STATE + 2
STRIP, SLOTS = 24, 5
STRIP_ROW = ROWS + 2 * HALO + 1
TOTAL_ROWS = STRIP_ROW + SLOTS + 1
DIRS = ((0, 1), (0, -1), (1, 0), (-1, 0))
SELF_COEF = (1.0 - 3.0 * DT) / (0.5 * DT)


def lane_roll(value, shift):
    if isinstance(shift, int):
        shift = shift % LANES
        return value if shift == 0 else pltpu.roll(value, shift, 1)
    return pltpu.roll(value, lax.rem(shift + LANES, LANES), 1)


def fluxes(u):
    n, fx, fy, fz = u
    n2 = n * n
    f2 = fx * fx + fy * fy + fz * fz
    q = jnp.sqrt(4.0 * n2 - 3.0 * jnp.minimum(f2, n2))
    h = 3.0 / (2.0 * n + q)
    diag = (q - n) * (1.0 / 3.0)
    gx, gy, gz = h * fx, h * fy, h * fz
    pxy, pxz, pyz = gx * fy, gx * fz, gy * fz
    flux_x = (fx, gx * fx + diag, pxy, pxz)
    flux_y = (fy, pxy, gy * fy + diag, pyz)
    flux_z = (fz, pxz, pyz, gz * fz + diag)
    here = []
    for c in range(4):
        side = lane_roll(u[c] - flux_y[c], -1) + lane_roll(u[c] + flux_y[c], 1)
        side = side + pltpu.roll(u[c] - flux_z[c], DEPTH - 1, 0) + pltpu.roll(u[c] + flux_z[c], 1, 0)
        here.append(SELF_COEF * u[c] + side)
    to_lower = [u[c] - flux_x[c] for c in range(4)]
    to_upper = [u[c] + flux_x[c] for c in range(4)]
    return here, to_lower, to_upper


def photochemistry(n1, n2, x0, dens):
    dn = DT * dens
    rec = ALPHA * dn
    m1, m2 = (DT * SIGMA[0]) * n1, (DT * SIGMA[1]) * n2
    x = x0
    for step in range(CHEM_ITERS):
        u = dn * (1.0 - x)
        d1, d2 = 1.0 + SIGMA[0] * u, 1.0 + SIGMA[1] * u
        both = d1 * d2
        gamma = m1 * d2 + m2 * d1
        top = x0 * both + gamma
        bottom = both * (1.0 + rec * x) + gamma
        if step < CHEM_ITERS - 1:
            x = top / bottom
        else:
            inverse = 1.0 / (both * bottom)
            x = top * (both * inverse)
            per_both = bottom * inverse
    return d2 * per_both, d1 * per_both, x


def kernel(
    rad_hbm, ion_hbm, dens_hbm, lum_hbm, cell_hbm, offset_hbm, count_hbm, rad_out, ion_out,
    raw, lum, cell, offset, count, own, own_e, ions, flux_buf, strips, final,
    y_send, d_send, e_send, x_recv, y_recv, d_recv, e_recv, in_sem, send_sem, recv_sem,
):
    nx, ny = lax.axis_size("gx"), lax.axis_size("gy")
    me_x, me_y = lax.axis_index("gx"), lax.axis_index("gy")

    def device(direction):
        dx, dy = direction
        return (lax.rem(me_x + dx + nx, nx), lax.rem(me_y + dy + ny, ny))

    copies_in = [
        pltpu.make_async_copy(src, dst, in_sem.at[i])
        for i, (src, dst) in enumerate(
            (
                (rad_hbm, raw.at[pl.ds(0, FIELDS)]),
                (ion_hbm, raw.at[ION]),
                (dens_hbm, raw.at[DENS]),
                (lum_hbm, lum),
                (cell_hbm, cell),
                (offset_hbm, offset),
                (count_hbm, count),
            )
        )
    ]
    for copy in copies_in:
        copy.start()
    barrier = pltpu.get_barrier_semaphore()
    for direction in DIRS:
        pl.semaphore_signal(barrier, inc=1, device_id=device(direction), device_id_type=MESH)

    lane = lax.broadcasted_iota(jnp.int32, (DEPTH, LANES), 1)
    slot_col = lax.rem(lane, STRIP)
    zeros = jnp.zeros((DEPTH, LANES), F32)

    def between(position, low, width):
        return (position >= low) & (position < low + width)

    def send(src, dst, index, direction):
        copy = pltpu.make_async_remote_copy(
            src_ref=src,
            dst_ref=dst,
            send_sem=send_sem.at[index],
            recv_sem=recv_sem.at[index],
            device_id=device(direction),
            device_id_type=MESH,
        )
        copy.start()
        return copy

    for copy in copies_in[:3]:
        copy.wait()

    for x in range(ROWS):
        for a in range(STATE):
            own[a, x + HALO] = raw[a, pl.ds(x, DEPTH, stride=ROWS), :]

    for copy in copies_in[3:]:
        copy.wait()
    stars = lum.shape[1]
    live = (lax.broadcasted_iota(jnp.int32, (1, stars), 1) < count[...]).astype(F32)

    def corner_weight(axis, position, wrapped=False):
        low, frac = cell[axis], offset[axis]
        high = low + 1
        if wrapped:
            high = jnp.where(high >= DEPTH, high - DEPTH, high)
        return jnp.where(low == position, 1.0 - frac, 0.0) + jnp.where(high == position, frac, 0.0)

    z_at = lax.broadcasted_iota(jnp.int32, (DEPTH, stars), 0)
    weight_z = corner_weight(2, z_at, True)
    strength = [weight_z * (lum[g : g + 1, :] * live * DT) for g in range(2)]
    y_at = lax.broadcasted_iota(jnp.int32, (LANES, stars), 0)
    weight_y = corner_weight(1, y_at)
    weight_x = corner_weight(0, y_at)
    over_y = corner_weight(1, jnp.full((1, stars), LANES, jnp.int32))
    weight_rows = [corner_weight(0, jnp.full((1, stars), x, jnp.int32)) for x in range(ROWS + 1)]
    spread = [strength[g] * weight_rows[x] for g in range(2) for x in range(ROWS + 1)]
    contract = functools.partial(
        lax.dot_general,
        dimension_numbers=(((1,), (1,)), ((), ())),
        precision=lax.Precision.HIGHEST,
        preferred_element_type=F32,
    )
    deposit = contract(jnp.concatenate(spread, axis=0), weight_y)
    column = contract(jnp.concatenate([s * over_y for s in strength], axis=0), weight_x)
    moved = [[None] * (ROWS + 1) for _ in range(2)]
    for g in range(2):
        for x in range(ROWS + 1):
            at = (g * (ROWS + 1) + x) * DEPTH
            row = deposit[at : at + DEPTH]
            own_e[g, HALO + x] = row
            over = lane_roll(column[g * DEPTH : (g + 1) * DEPTH], LANES - 1 - x)
            moved[g][x] = jnp.where(lane == LANES - 1, over, lane_roll(row, -1))

    def array_row(a, r):
        return own[a, r] if a < STATE else own_e[a - STATE, r]

    for a in range(ARRAYS):
        for side in range(2):
            total = zeros
            for x in range(ROWS + (a >= STATE)):
                base = 4 * (x + HALO) + 4 * ((x + HALO) // SLOTS)
                if side == 1:
                    piece = lane_roll(array_row(a, x + HALO), base)
                else:
                    row = array_row(a, x + HALO) if a < STATE else moved[a - STATE][x]
                    piece = lane_roll(row, base + 4)
                total = jnp.where(between(lane, base, 4), piece, total)
            y_send[side, a] = total

    for g in range(2):
        strip = []
        for v in range(SLOTS):
            total = zeros
            for s in range(SLOTS):
                x, at = SLOTS * s + v - HALO, STRIP * s
                if 0 <= x <= ROWS:
                    total = jnp.where(between(lane, at + 1, 8), lane_roll(moved[g][x], at + 9), total)
                    total = jnp.where(between(lane, at + 16, 8), lane_roll(own_e[g, x + HALO], at + 16), total)
            strip.append(total)
            strips[STATE + g, v] = total
        for i, (first, target) in enumerate(((ROWS + 1, 1), (HALO, ROWS + HALO))):
            total = zeros
            for j in range(HALO):
                e_send[i, g, j] = own_e[g, first + j]
                s, v = divmod(first + j, SLOTS)
                place = (target + j) % SLOTS
                piece = lane_roll(strip[v], STRIP * (place - s))
                total = jnp.where(between(lane, STRIP * place, STRIP), piece, total)
            e_send[i, g, HALO] = total

    pl.semaphore_wait(barrier, len(DIRS))
    y_copies = [send(y_send.at[i], y_recv.at[i], i, DIRS[i]) for i in range(2)]
    x_copies = []
    for i in range(2):
        rows = own.at[:, pl.ds(HALO if i else ROWS, HALO)]
        x_copies.append(send(rows, x_recv.at[i], 2 + i, DIRS[2 + i]))
        x_copies.append(send(e_send.at[i], e_recv.at[i], 4 + i, DIRS[2 + i]))

    def store_flux(k, g, r, u):
        here, to_lower, to_upper = fluxes(u)
        for c in range(4):
            flux_buf[k, g, c, r] = here[c]
            flux_buf[k, g, 4 + c, r] = to_lower[c]
            flux_buf[k, g, 8 + c, r] = to_upper[c]

    def substep(k, r):
        u = []
        for g in range(2):
            for c in range(4):
                total = flux_buf[k - 1, g, c, r] + (flux_buf[k - 1, g, 4 + c, r + 1] + flux_buf[k - 1, g, 8 + c, r - 1])
                u.append((0.5 * DT) * total)
            u[4 * g] = u[4 * g] + own_e[g, r]
        att1, att2, x = photochemistry(u[0], u[4], ions[k - 1, r], ions[SUBSTEPS, r])
        u = [value * (att1 if i < 4 else att2) for i, value in enumerate(u)]
        if k < SUBSTEPS:
            store_flux(k, 0, r, u[:4])
            store_flux(k, 1, r, u[4:])
            ions[k, r] = x
        else:
            for i in range(FIELDS):
                final[i, r] = u[i]
            final[ION, r] = x

    for r in range(HALO, HALO + ROWS):
        ions[0, r] = own[ION, r]
        ions[SUBSTEPS, r] = own[DENS, r]
        for g in range(2):
            store_flux(0, g, r, [own[4 * g + c, r] for c in range(4)])
    for k in range(1, SUBSTEPS + 1):
        for r in range(HALO + k, HALO + ROWS - k):
            substep(k, r)

    def pack_strip(row, s, old):
        at = STRIP * s
        new = jnp.where(between(lane, at, 8), lane_roll(row, at + 8), old)
        return jnp.where(between(lane, at + 16, 8), lane_roll(row, at + 16), new)

    for a in range(STATE):
        for v in range(SLOTS):
            total = zeros
            for s in range(SLOTS):
                if HALO <= SLOTS * s + v < HALO + ROWS:
                    total = pack_strip(own[a, SLOTS * s + v], s, total)
            strips[a, v] = total

    def corner(value, dx, place, last_row):
        at = STRIP * place
        if dx > 0:
            out = jnp.where(between(lane, at, 16), lane_roll(value, at - 76), 0.0)
            if last_row:
                out = jnp.where(between(lane, at + 16, 4), lane_roll(value, at - 80), out)
            return out
        out = jnp.where(between(lane, at, 4), lane_roll(value, at - 16), 0.0)
        return jnp.where(between(lane, at + 4, 12), lane_roll(value, at - 20), out)

    for copy in y_copies:
        copy.wait_recv()
    for i in range(2):
        for side in range(2):
            for part in range(3):
                total = zeros
                for place in range(min(SLOTS, ARRAYS - SLOTS * part)):
                    a = SLOTS * part + place
                    total = total + corner(y_recv[side, a], 1 if i == 0 else -1, place, a >= STATE)
                d_send[i, side, part] = total
    d_copies = [send(d_send.at[i], d_recv.at[i], 6 + i, DIRS[2 + i]) for i in range(2)]

    def add_edges(lower, upper, v, deposits, value, mask):
        first = 13 if deposits else 12
        lower_mask, upper_mask = between(slot_col, first, 4), between(slot_col, 8, 4)
        if mask is not None:
            lower_mask, upper_mask = lower_mask & mask, upper_mask & mask
        other = value if deposits else 0.0
        value = jnp.where(lower_mask, lane_roll(lower, first - 4 * v) + other, value)
        return jnp.where(upper_mask, lane_roll(upper, 8 - 4 * v) + other, value)

    for a in range(ARRAYS):
        for v in range(SLOTS):
            strips[a, v] = add_edges(y_recv[0, a], y_recv[1, a], v, a >= STATE, strips[a, v], None)

    for copy in x_copies:
        copy.wait_recv()
    for j in range(HALO):
        for i, r in ((0, j), (1, ROWS + HALO + j)):
            ions[0, r] = x_recv[i, ION, j]
            ions[SUBSTEPS, r] = x_recv[i, DENS, j]
            for g in range(2):
                store_flux(0, g, r, [x_recv[i, 4 * g + c, j] for c in range(4)])
    for g in range(2):
        for j in range(HALO):
            low, high = 1 + j, ROWS + HALO + j
            if j < HALO - 1:
                own_e[g, low] = e_recv[0, g, j]
            else:
                own_e[g, low] = own_e[g, low] + e_recv[0, g, j]
            if j == 0:
                own_e[g, high] = own_e[g, high] + e_recv[1, g, j]
            else:
                own_e[g, high] = e_recv[1, g, j]
    for k in range(1, SUBSTEPS + 1):
        for i in range(HALO):
            substep(k, k + i)
            substep(k, ROWS + HALO - k + i)

    outer = (lane < STRIP) | between(lane, STRIP * (SLOTS - 1), STRIP)
    for a in range(STATE):
        for v in range(HALO):
            value = pack_strip(x_recv[0, a, v], 0, strips[a, v])
            strips[a, v] = pack_strip(x_recv[1, a, v], SLOTS - 1, value)
    for g in range(2):
        for v in range(SLOTS):
            last = STRIP * (SLOTS - 1)
            value = strips[STATE + g, v]
            value = value + jnp.where(lane < STRIP, lane_roll(e_recv[0, g, HALO], -STRIP * v), 0.0)
            piece = lane_roll(e_recv[1, g, HALO], last - STRIP * v)
            strips[STATE + g, v] = value + jnp.where(between(lane, last, STRIP), piece, 0.0)
    for copy in d_copies:
        copy.wait_recv()

    def unslot(value, place, slot, width):
        return jnp.where(between(lane, STRIP * slot, width), lane_roll(value, STRIP * (slot - place)), 0.0)

    for a in range(ARRAYS):
        part, place = divmod(a, SLOTS)
        deposits = a >= STATE
        edges = []
        for side in range(2):
            low = unslot(d_recv[0, side, part], place, 0, 20 if deposits else 16)
            edges.append(low + unslot(d_recv[1, side, part], place, SLOTS - 1, 16))
        for v in range(SLOTS):
            if not deposits and v == SLOTS - 1:
                continue
            value = add_edges(edges[0], edges[1], v, deposits, strips[a, v], outer)
            if deposits:
                own_e[a - STATE, STRIP_ROW + v] = value
            else:
                strips[a, v] = value

    def wrap_strips(k):
        for g in range(2):
            for c in range(4):
                flux_buf[k, g, 4 + c, STRIP_ROW + SLOTS] = lane_roll(flux_buf[k, g, 4 + c, STRIP_ROW], -STRIP)
                flux_buf[k, g, 8 + c, STRIP_ROW - 1] = lane_roll(flux_buf[k, g, 8 + c, STRIP_ROW + SLOTS - 1], STRIP)

    for v in range(SLOTS):
        ions[0, STRIP_ROW + v] = strips[ION, v]
        ions[SUBSTEPS, STRIP_ROW + v] = strips[DENS, v]
        for g in range(2):
            store_flux(0, g, STRIP_ROW + v, [strips[4 * g + c, v] for c in range(4)])
    for k in range(1, SUBSTEPS + 1):
        wrap_strips(k - 1)

        for v in range(SLOTS):
            substep(k, STRIP_ROW + v)

    for x in range(ROWS):
        s, v = divmod(x + HALO, SLOTS)
        for a in range(FIELDS + 1):
            edge_cols = final[a, STRIP_ROW + v]
            value = final[a, x + HALO]
            value = jnp.where(lane < HALO, lane_roll(edge_cols, -16 - STRIP * s), value)
            value = jnp.where(lane >= LANES - HALO, lane_roll(edge_cols, -8 - STRIP * s), value)
            if a < FIELDS:
                rad_out[a, pl.ds(x, DEPTH, stride=ROWS), :] = value
            else:
                ion_out[pl.ds(x, DEPTH, stride=ROWS), :] = value
    for copy in y_copies + x_copies + d_copies:
        copy.wait_send()


def on_device(radiation, ion_fraction, density, star_lum, star_cell, star_offset, star_count):
    groups, comps, depth, rows, lanes = radiation.shape
    assert (groups * comps, depth, rows, lanes) == (FIELDS, DEPTH, ROWS, LANES)
    stars = star_lum.shape[3]
    plane = (depth * rows, lanes)
    vmem = lambda *shape: pltpu.VMEM(shape + (DEPTH, LANES), F32)
    hbm = lambda value: pltpu.with_memory_space_constraint(value, pltpu.HBM)
    rad, ion = pl.pallas_call(
        kernel,
        out_shape=(
            jax.ShapeDtypeStruct((FIELDS,) + plane, F32),
            jax.ShapeDtypeStruct(plane, F32),
        ),
        in_specs=[pl.BlockSpec(memory_space=pltpu.HBM)] * 7,
        out_specs=(pl.BlockSpec(memory_space=pltpu.VMEM),) * 2,
        scratch_shapes=[
            pltpu.VMEM((STATE,) + plane, F32),
            pltpu.VMEM((2, stars), F32),
            pltpu.VMEM((3, 1, stars), jnp.int32),
            pltpu.VMEM((3, 1, stars), F32),
            pltpu.VMEM((1, 1), jnp.int32),
            vmem(STATE, ROWS + 2 * HALO),
            vmem(2, TOTAL_ROWS),
            vmem(SUBSTEPS + 1, TOTAL_ROWS),
            vmem(SUBSTEPS, 2, 12, TOTAL_ROWS),
            vmem(ARRAYS, SLOTS),
            vmem(FIELDS + 1, TOTAL_ROWS),
            vmem(2, ARRAYS),
            vmem(2, 2, 3),
            vmem(2, 2, HALO + 1),
            vmem(2, STATE, HALO),
            vmem(2, ARRAYS),
            vmem(2, 2, 3),
            vmem(2, 2, HALO + 1),
            pltpu.SemaphoreType.DMA((7,)),
            pltpu.SemaphoreType.DMA((8,)),
            pltpu.SemaphoreType.DMA((8,)),
        ],
        compiler_params=pltpu.CompilerParams(
            collective_id=0, has_side_effects=True, vmem_limit_bytes=40 * 1024 * 1024
        ),
    )(
        hbm(radiation.reshape((FIELDS,) + plane)),
        hbm(ion_fraction.reshape(plane)),
        hbm(density.reshape(plane)),
        hbm(star_lum[0, 0]),
        hbm(star_cell.reshape(3, 1, stars)),
        hbm(star_offset.reshape(3, 1, stars)),
        star_count,
    )
    return rad.reshape(radiation.shape), ion.reshape(ion_fraction.shape)


def solution(mesh):
    return jax.shard_map(
        on_device,
        mesh=mesh,
        in_specs=(
            P(None, None, None, "gx", "gy"),
            P(None, "gx", "gy"),
            P(None, "gx", "gy"),
            P("gx", "gy", None, None),
            P("gx", "gy", None, None),
            P("gx", "gy", None, None),
            P("gx", "gy"),
        ),
        out_specs=(P(None, None, None, "gx", "gy"), P(None, "gx", "gy")),
        check_vma=False,
    )
```

```python
import functools

import jax
import jax.numpy as jnp
from jax import lax
from jax.experimental import pallas as pl
from jax.experimental.pallas import tpu as pltpu
from jax.sharding import PartitionSpec as P

SUBSTEPS = 4
CHEM_ITERS = 3
DT = 0.3
ALPHA = 0.4
SIGMA = (1.5, 0.5)

MESH = pl.DeviceIdType.MESH
F32 = jnp.float32

ROWS, DEPTH, LANES = 16, 8, 128
HALO = SUBSTEPS
FIELDS = 8
ION, DENS, STATE = 8, 9, 10
ARRAYS = STATE + 2
STRIP, SLOTS = 24, 5
STRIP_ROW = ROWS + 2 * HALO + 1
TOTAL_ROWS = STRIP_ROW + SLOTS + 1
DIRS = ((0, 1), (0, -1), (1, 0), (-1, 0))
SELF_COEF = (1.0 - 3.0 * DT) / (0.5 * DT)


def lane_roll(value, shift):
    if isinstance(shift, int):
        shift = shift % LANES
        return value if shift == 0 else pltpu.roll(value, shift, 1)
    return pltpu.roll(value, lax.rem(shift + LANES, LANES), 1)


def fluxes(u):
    n, fx, fy, fz = u
    n2 = n * n
    f2 = fx * fx + fy * fy + fz * fz
    q = jnp.sqrt(4.0 * n2 - 3.0 * jnp.minimum(f2, n2))
    h = 3.0 / (2.0 * n + q)
    diag = (q - n) * (1.0 / 3.0)
    gx, gy, gz = h * fx, h * fy, h * fz
    pxy, pxz, pyz = gx * fy, gx * fz, gy * fz
    flux_x = (fx, gx * fx + diag, pxy, pxz)
    flux_y = (fy, pxy, gy * fy + diag, pyz)
    flux_z = (fz, pxz, pyz, gz * fz + diag)
    here = []
    for c in range(4):
        side = lane_roll(u[c] - flux_y[c], -1) + lane_roll(u[c] + flux_y[c], 1)
        side = side + pltpu.roll(u[c] - flux_z[c], DEPTH - 1, 0) + pltpu.roll(u[c] + flux_z[c], 1, 0)
        here.append(SELF_COEF * u[c] + side)
    to_lower = [u[c] - flux_x[c] for c in range(4)]
    to_upper = [u[c] + flux_x[c] for c in range(4)]
    return here, to_lower, to_upper


def photochemistry(n1, n2, x0, dens):
    dn = DT * dens
    rec = ALPHA * dn
    m1, m2 = (DT * SIGMA[0]) * n1, (DT * SIGMA[1]) * n2
    x = x0
    for step in range(CHEM_ITERS):
        u = dn * (1.0 - x)
        d1, d2 = 1.0 + SIGMA[0] * u, 1.0 + SIGMA[1] * u
        both = d1 * d2
        gamma = m1 * d2 + m2 * d1
        top = x0 * both + gamma
        bottom = both * (1.0 + rec * x) + gamma
        if step < CHEM_ITERS - 1:
            x = top / bottom
        else:
            inverse = 1.0 / (both * bottom)
            x = top * (both * inverse)
            per_both = bottom * inverse
    return d2 * per_both, d1 * per_both, x


def kernel(
    rad_hbm, ion_hbm, dens_hbm, lum_hbm, cell_hbm, offset_hbm, count_hbm, final,
    raw, lum, cell, offset, count, table, own, own_e, ions, flux_buf, strips,
    y_send, d_send, x_recv, y_recv, d_recv, table_recv, in_sem, send_sem, recv_sem,
):
    nx, ny = lax.axis_size("gx"), lax.axis_size("gy")
    me_x, me_y = lax.axis_index("gx"), lax.axis_index("gy")

    def device(direction):
        dx, dy = direction
        return (lax.rem(me_x + dx + nx, nx), lax.rem(me_y + dy + ny, ny))

    copies_in = [
        pltpu.make_async_copy(src, dst, in_sem.at[i])
        for i, (src, dst) in enumerate(
            (
                (lum_hbm, lum),
                (cell_hbm, cell),
                (offset_hbm, offset),
                (count_hbm, count),
                (rad_hbm, raw.at[pl.ds(0, FIELDS)]),
                (ion_hbm, raw.at[ION]),
                (dens_hbm, raw.at[DENS]),
            )
        )
    ]
    for copy in copies_in:
        copy.start()
    barrier = pltpu.get_barrier_semaphore()
    for direction in DIRS:
        pl.semaphore_signal(barrier, inc=1, device_id=device(direction), device_id_type=MESH)

    lane = lax.broadcasted_iota(jnp.int32, (DEPTH, LANES), 1)
    slot_col = lax.rem(lane, STRIP)
    zeros = jnp.zeros((DEPTH, LANES), F32)

    def between(position, low, width):
        return (position >= low) & (position < low + width)

    def send(src, dst, index, direction):
        copy = pltpu.make_async_remote_copy(
            src_ref=src,
            dst_ref=dst,
            send_sem=send_sem.at[index],
            recv_sem=recv_sem.at[index],
            device_id=device(direction),
            device_id_type=MESH,
        )
        copy.start()
        return copy

    for copy in copies_in[:4]:
        copy.wait()
    stars = lum.shape[1]
    live = (lax.broadcasted_iota(jnp.int32, (1, stars), 1) < count[...]).astype(F32)
    for g in range(2):
        table[g : g + 1, :] = lum[g : g + 1, :] * live * DT
    for axis in range(3):
        table[2 + axis : 3 + axis, :] = cell[axis].astype(F32)
        table[5 + axis : 6 + axis, :] = offset[axis]
    contract = functools.partial(
        lax.dot_general,
        dimension_numbers=(((1,), (1,)), ((), ())),
        precision=lax.Precision.HIGHEST,
        preferred_element_type=F32,
    )

    def deposits(stars_at, rows):
        def corner_weight(axis, position, wrapped=False):
            low, frac = stars_at[2 + axis : 3 + axis, :], stars_at[5 + axis : 6 + axis, :]
            high = low + 1.0
            if wrapped:
                high = jnp.where(high >= DEPTH, high - DEPTH, high)
            return jnp.where(low == position, 1.0 - frac, 0.0) + jnp.where(high == position, frac, 0.0)

        z_at = lax.broadcasted_iota(jnp.int32, (DEPTH, stars), 0).astype(F32)
        y_at = lax.broadcasted_iota(jnp.int32, (LANES, stars), 0).astype(F32)
        weight_z = corner_weight(2, z_at, True)
        strength = [weight_z * stars_at[g : g + 1, :] for g in range(2)]
        weight_rows = [corner_weight(0, jnp.full((1, stars), x, F32)) for x in rows]
        spread = [strength[g] * weight for g in range(2) for weight in weight_rows]
        over_y = corner_weight(1, jnp.full((1, stars), LANES, F32))
        deposit = contract(jnp.concatenate(spread, axis=0), corner_weight(1, y_at))
        column = contract(jnp.concatenate([s * over_y for s in strength], axis=0), corner_weight(0, y_at))
        here, moved = [], []
        for g in range(2):
            for i, x in enumerate(rows):
                at = (g * len(rows) + i) * DEPTH
                row = deposit[at : at + DEPTH]
                over = lane_roll(column[g * DEPTH : (g + 1) * DEPTH], LANES - 1 - x)
                here.append(row)
                moved.append(jnp.where(lane == LANES - 1, over, lane_roll(row, -1)))
        return here, moved

    def strip_of_deposit(row, moved, s, old):
        at = STRIP * s
        old = old + jnp.where(between(lane, at + 1, 8), lane_roll(moved, at + 9), 0.0)
        return old + jnp.where(between(lane, at + 16, 8), lane_roll(row, at + 16), 0.0)

    here, moved_rows = deposits(table, range(ROWS + 1))
    moved = [moved_rows[: ROWS + 1], moved_rows[ROWS + 1 :]]
    for g in range(2):
        for x in range(ROWS + 1):
            own_e[g, HALO + x] = here[g * (ROWS + 1) + x]

    for copy in copies_in[4:]:
        copy.wait()

    for x in range(ROWS):
        for a in range(STATE):
            own[a, x + HALO] = raw[a, pl.ds(x, DEPTH, stride=ROWS), :]

    def array_row(a, r):
        return own[a, r] if a < STATE else own_e[a - STATE, r]

    for a in range(ARRAYS):
        for side in range(2):
            total = zeros
            for x in range(ROWS + (a >= STATE)):
                base = 4 * (x + HALO) + 4 * ((x + HALO) // SLOTS)
                if side == 1:
                    piece = lane_roll(array_row(a, x + HALO), base)
                else:
                    row = array_row(a, x + HALO) if a < STATE else moved[a - STATE][x]
                    piece = lane_roll(row, base + 4)
                total = jnp.where(between(lane, base, 4), piece, total)
            y_send[side, a] = total

    pl.semaphore_wait(barrier, len(DIRS))
    y_copies = [send(y_send.at[i], y_recv.at[i], i, DIRS[i]) for i in range(2)]
    table_copies = [send(table, table_recv.at[i], 4 + i, DIRS[2 + i]) for i in range(2)]
    x_copies = []
    for i in range(2):
        rows = own.at[:, pl.ds(HALO if i else ROWS, HALO)]
        x_copies.append(send(rows, x_recv.at[i], 2 + i, DIRS[2 + i]))

    def store_flux(k, g, r, u):
        here, to_lower, to_upper = fluxes(u)
        for c in range(4):
            flux_buf[k, g, c, r] = here[c]
            flux_buf[k, g, 4 + c, r] = to_lower[c]
            flux_buf[k, g, 8 + c, r] = to_upper[c]

    def substep(k, r):
        u = []
        for g in range(2):
            for c in range(4):
                total = flux_buf[k - 1, g, c, r] + (flux_buf[k - 1, g, 4 + c, r + 1] + flux_buf[k - 1, g, 8 + c, r - 1])
                u.append((0.5 * DT) * total)
            u[4 * g] = u[4 * g] + own_e[g, r]
        att1, att2, x = photochemistry(u[0], u[4], ions[k - 1, r], ions[SUBSTEPS, r])
        u = [value * (att1 if i < 4 else att2) for i, value in enumerate(u)]
        if k < SUBSTEPS:
            store_flux(k, 0, r, u[:4])
            store_flux(k, 1, r, u[4:])
            ions[k, r] = x
        else:
            for i in range(FIELDS):
                final[i, r] = u[i]
            final[ION, r] = x

    for g in range(2):
        for v in range(SLOTS):
            total = zeros
            for s in range(SLOTS):
                x = SLOTS * s + v - HALO
                if 0 <= x <= ROWS:
                    total = strip_of_deposit(own_e[g, x + HALO], moved[g][x], s, total)
            strips[STATE + g, v] = total

    for r in range(HALO, HALO + ROWS):
        ions[0, r] = own[ION, r]
        ions[SUBSTEPS, r] = own[DENS, r]
        for g in range(2):
            store_flux(0, g, r, [own[4 * g + c, r] for c in range(4)])
    for k in range(1, SUBSTEPS + 1):
        for r in range(HALO + k, HALO + ROWS - k):
            substep(k, r)

    def pack_strip(row, s, old):
        at = STRIP * s
        new = jnp.where(between(lane, at, 8), lane_roll(row, at + 8), old)
        return jnp.where(between(lane, at + 16, 8), lane_roll(row, at + 16), new)

    for a in range(STATE):
        for v in range(SLOTS):
            total = zeros
            for s in range(SLOTS):
                if HALO <= SLOTS * s + v < HALO + ROWS:
                    total = pack_strip(own[a, SLOTS * s + v], s, total)
            strips[a, v] = total

    def corner(value, dx, place, last_row):
        at = STRIP * place
        if dx > 0:
            out = jnp.where(between(lane, at, 16), lane_roll(value, at - 76), 0.0)
            if last_row:
                out = jnp.where(between(lane, at + 16, 4), lane_roll(value, at - 80), out)
            return out
        out = jnp.where(between(lane, at, 4), lane_roll(value, at - 16), 0.0)
        return jnp.where(between(lane, at + 4, 12), lane_roll(value, at - 20), out)

    for copy in y_copies:
        copy.wait_recv()
    for i in range(2):
        for side in range(2):
            for part in range(3):
                total = zeros
                for place in range(min(SLOTS, ARRAYS - SLOTS * part)):
                    a = SLOTS * part + place
                    total = total + corner(y_recv[side, a], 1 if i == 0 else -1, place, a >= STATE)
                d_send[i, side, part] = total
    d_copies = [send(d_send.at[i], d_recv.at[i], 6 + i, DIRS[2 + i]) for i in range(2)]

    def add_edges(lower, upper, v, deposits, value, mask):
        first = 13 if deposits else 12
        lower_mask, upper_mask = between(slot_col, first, 4), between(slot_col, 8, 4)
        if mask is not None:
            lower_mask, upper_mask = lower_mask & mask, upper_mask & mask
        other = value if deposits else 0.0
        value = jnp.where(lower_mask, lane_roll(lower, first - 4 * v) + other, value)
        return jnp.where(upper_mask, lane_roll(upper, 8 - 4 * v) + other, value)

    for a in range(ARRAYS):
        for v in range(SLOTS):
            strips[a, v] = add_edges(y_recv[0, a], y_recv[1, a], v, a >= STATE, strips[a, v], None)

    for copy in table_copies:
        copy.wait_recv()
    for i, rows in enumerate((range(ROWS - HALO + 1, ROWS + 1), range(HALO - 1))):
        from_x, from_x_moved = deposits(table_recv.at[i], rows)
        for g in range(2):
            for j, x in enumerate(rows):
                r = x + HALO + (ROWS if i else -ROWS)
                s, v = divmod(r, SLOTS)
                row, row_moved = from_x[g * len(rows) + j], from_x_moved[g * len(rows) + j]
                own_e[g, r] = row + own_e[g, r] if r in (HALO, ROWS + HALO) else row
                strips[STATE + g, v] = strip_of_deposit(row, row_moved, s, strips[STATE + g, v])

    for copy in x_copies:
        copy.wait_recv()
    for j in range(HALO):
        for i, r in ((0, j), (1, ROWS + HALO + j)):
            ions[0, r] = x_recv[i, ION, j]
            ions[SUBSTEPS, r] = x_recv[i, DENS, j]
            for g in range(2):
                store_flux(0, g, r, [x_recv[i, 4 * g + c, j] for c in range(4)])

    outer = (lane < STRIP) | between(lane, STRIP * (SLOTS - 1), STRIP)
    for a in range(STATE):
        for v in range(HALO):
            value = pack_strip(x_recv[0, a, v], 0, strips[a, v])
            strips[a, v] = pack_strip(x_recv[1, a, v], SLOTS - 1, value)
    for copy in d_copies:
        copy.wait_recv()

    def unslot(value, place, slot, width):
        return jnp.where(between(lane, STRIP * slot, width), lane_roll(value, STRIP * (slot - place)), 0.0)

    for a in range(ARRAYS):
        part, place = divmod(a, SLOTS)
        deposits = a >= STATE
        edges = []
        for side in range(2):
            low = unslot(d_recv[0, side, part], place, 0, 20 if deposits else 16)
            edges.append(low + unslot(d_recv[1, side, part], place, SLOTS - 1, 16))
        for v in range(SLOTS):
            if not deposits and v == SLOTS - 1:
                continue
            value = add_edges(edges[0], edges[1], v, deposits, strips[a, v], outer)
            if deposits:
                own_e[a - STATE, STRIP_ROW + v] = value
            else:
                strips[a, v] = value

    def wrap_strips(k):
        for g in range(2):
            for c in range(4):
                flux_buf[k, g, 4 + c, STRIP_ROW + SLOTS] = lane_roll(flux_buf[k, g, 4 + c, STRIP_ROW], -STRIP)
                flux_buf[k, g, 8 + c, STRIP_ROW - 1] = lane_roll(flux_buf[k, g, 8 + c, STRIP_ROW + SLOTS - 1], STRIP)

    for v in range(SLOTS):
        ions[0, STRIP_ROW + v] = strips[ION, v]
        ions[SUBSTEPS, STRIP_ROW + v] = strips[DENS, v]
        for g in range(2):
            store_flux(0, g, STRIP_ROW + v, [strips[4 * g + c, v] for c in range(4)])
    for k in range(1, SUBSTEPS + 1):
        for i in range(HALO):
            substep(k, k + i)
            substep(k, ROWS + HALO - k + i)
        wrap_strips(k - 1)

        for v in range(SLOTS):
            substep(k, STRIP_ROW + v)

    for copy in y_copies + table_copies + x_copies + d_copies:
        copy.wait_send()


def merge_kernel(final, rad_out, ion_out, raw_out, out_sem):
    lane = lax.broadcasted_iota(jnp.int32, (DEPTH, LANES), 1)
    copies = []
    for a in range(FIELDS + 1):
        for x in range(ROWS):
            s, v = divmod(x + HALO, SLOTS)
            edge_cols = final[a, STRIP_ROW + v]
            value = final[a, x + HALO]
            value = jnp.where(lane < HALO, lane_roll(edge_cols, -16 - STRIP * s), value)
            value = jnp.where(lane >= LANES - HALO, lane_roll(edge_cols, -8 - STRIP * s), value)
            raw_out[a, pl.ds(x, DEPTH, stride=ROWS), :] = value
        target = rad_out.at[a] if a < FIELDS else ion_out
        copies.append(pltpu.make_async_copy(raw_out.at[a], target, out_sem.at[a]))
        copies[-1].start()
    for copy in copies:
        copy.wait()


def on_device(radiation, ion_fraction, density, star_lum, star_cell, star_offset, star_count):
    groups, comps, depth, rows, lanes = radiation.shape
    assert (groups * comps, depth, rows, lanes) == (FIELDS, DEPTH, ROWS, LANES)
    stars = star_lum.shape[3]
    plane = (depth * rows, lanes)
    vmem = lambda *shape: pltpu.VMEM(shape + (DEPTH, LANES), F32)
    hbm = lambda value: pltpu.with_memory_space_constraint(value, pltpu.HBM)
    final = pl.pallas_call(
        kernel,
        out_shape=jax.ShapeDtypeStruct((FIELDS + 1, TOTAL_ROWS, DEPTH, LANES), F32),
        in_specs=[pl.BlockSpec(memory_space=pltpu.HBM)] * 7,
        out_specs=pl.BlockSpec(memory_space=pltpu.VMEM),
        scratch_shapes=[
            pltpu.VMEM((STATE,) + plane, F32),
            pltpu.VMEM((2, stars), F32),
            pltpu.VMEM((3, 1, stars), jnp.int32),
            pltpu.VMEM((3, 1, stars), F32),
            pltpu.VMEM((1, 1), jnp.int32),
            pltpu.VMEM((8, stars), F32),
            vmem(STATE, ROWS + 2 * HALO),
            vmem(2, TOTAL_ROWS),
            vmem(SUBSTEPS + 1, TOTAL_ROWS),
            vmem(SUBSTEPS, 2, 12, TOTAL_ROWS),
            vmem(ARRAYS, SLOTS),
            vmem(2, ARRAYS),
            vmem(2, 2, 3),
            vmem(2, STATE, HALO),
            vmem(2, ARRAYS),
            vmem(2, 2, 3),
            pltpu.VMEM((2, 8, stars), F32),
            pltpu.SemaphoreType.DMA((7,)),
            pltpu.SemaphoreType.DMA((8,)),
            pltpu.SemaphoreType.DMA((8,)),
        ],
        compiler_params=pltpu.CompilerParams(
            collective_id=0, has_side_effects=True, vmem_limit_bytes=40 * 1024 * 1024
        ),
    )(
        hbm(radiation.reshape((FIELDS,) + plane)),
        hbm(ion_fraction.reshape(plane)),
        hbm(density.reshape(plane)),
        hbm(star_lum[0, 0]),
        hbm(star_cell.reshape(3, 1, stars)),
        hbm(star_offset.reshape(3, 1, stars)),
        star_count,
    )
    rad, ion = pl.pallas_call(
        merge_kernel,
        out_shape=(
            jax.ShapeDtypeStruct((FIELDS,) + plane, F32),
            jax.ShapeDtypeStruct(plane, F32),
        ),
        in_specs=[pl.BlockSpec(memory_space=pltpu.VMEM)],
        out_specs=(pl.BlockSpec(memory_space=pltpu.HBM),) * 2,
        scratch_shapes=[
            pltpu.VMEM((FIELDS + 1,) + plane, F32),
            pltpu.SemaphoreType.DMA((FIELDS + 1,)),
        ],
    )(pltpu.with_memory_space_constraint(final, pltpu.VMEM))
    return rad.reshape(radiation.shape), ion.reshape(ion_fraction.shape)


def solution(mesh):
    return jax.shard_map(
        on_device,
        mesh=mesh,
        in_specs=(
            P(None, None, None, "gx", "gy"),
            P(None, "gx", "gy"),
            P(None, "gx", "gy"),
            P("gx", "gy", None, None),
            P("gx", "gy", None, None),
            P("gx", "gy", None, None),
            P("gx", "gy"),
        ),
        out_specs=(P(None, None, None, "gx", "gy"), P(None, "gx", "gy")),
        check_vma=False,
    )
```
